32 devices in a mesh: groups: 2 (over y), expert: 16 (over z, x, core).
Axes of the slice: x: 2, y: 2, z: 4, core: 2. Of those that a mesh axis runs over, the one named last changes fastest.
Arguments:
- queries: bfloat16 [192, 6144], P(('groups', 'expert')), parts along dimension 0, may hold values from -8 to 8
- tree_key_value: bfloat16 [192, 2, 1024], P(('groups', 'expert')), parts along dimension 0, may hold values from -6 to 6
- key_value_cache: bfloat16 [32, 2, 512, 1024], P(('groups', 'expert')), parts along dimension 0, may hold values from -8 to 8
- lengths: int32 [32], P(('groups', 'expert')), parts along dimension 0, may hold values from 128 to 512, as said below
- parents: int32 [192], P(('groups', 'expert')), parts along dimension 0, may hold values from 0 to 4, as said below
- residual: bfloat16 [192, 6144], P(('groups', 'expert')), parts along dimension 0, may hold values from -6 to 6
- ffn_gain: bfloat16 [6144], replicated, may hold values from 0.099609375 to 1.8984375
- router: bfloat16 [6144, 4], replicated, may hold values from -0.078125 to 0.078125
- routes: int32 [192, 2], P(('groups', 'expert')), parts along dimension 0, may hold values from 0 to 3, all different within a row; in each aligned block of 6 rows (0 to 5, 6 to 11, ...) at most 4 rows name the same one
- gate_weight: bfloat16 [6144, 32768], P(None, 'expert'), may hold values from -0.078125 to 0.078125
- up_weight: bfloat16 [6144, 32768], P(None, 'expert'), may hold values from -0.078125 to 0.078125
- down_weight: bfloat16 [32768, 6144], P('expert'), may hold values from -0.0625 to 0.0625
- accepted: int32 [32], P(('groups', 'expert')), parts along dimension 0, may hold values from 0 to 5
- next_embed: bfloat16 [32, 6144], P(('groups', 'expert')), parts along dimension 0, may hold values from -6 to 6
- draft_fc: bfloat16 [12288, 6144], P('expert'), may hold values from -0.0546875 to 0.0546875
Outputs:
- layer_out: bfloat16 [192, 6144], P(('groups', 'expert')), parts along dimension 0
- draft_out: bfloat16 [32, 6144], P(('groups', 'expert')), parts along dimension 0
The draws below stay inside these ranges and needn't reach their ends.
There are 2 independent parts, one for each index of `groups`. The reference program is written for one: setup_inputs(seed, part) draws one part's arguments, and reference() takes and returns one part's arrays. A program takes and returns all parts, laid end to end along the dimension named above; an argument that names none is the same for every part. Nothing has to cross between parts.
Inputs may be any that keep to these rules, and one draw needn't show every extreme that they name: `lengths`: both ends are reached by some request. `parents`: entry i of a request's 6 entries names an earlier node as its parent; entry 0, the root, names itself. `routes`: among the rows of one device no expert is named more than 4 times, a bound that some block reaches.
All inputs are finite; a program needn't handle non-finite values.
Results may differ from the reference program's by a relative error of at most 0.0051.
Values may be sent and summed in bfloat16 or wider, within the bound.
A program may use at most 128 MiB of HBM per device.

```python
import math
import jax
import jax.numpy as jnp
import numpy as np
from jax import lax

D = 6144
QUERY_HEADS = 48
KEY_VALUE_HEADS = 8
HEAD_SIZE = 128
FF = 8192
EXPERTS = 4
TREE_NODES = 6
CACHE_SLOTS = 512
TOK_DEV = 6
CAP = 4
REQUEST_COUNT = 16
TREE_TOKENS = 96
N_EXPERT = 16


def draw_queries(key, part):
    own_key = jax.random.fold_in(key, 31)
    base_draw = jnp.clip(jax.random.normal(own_key, (TREE_TOKENS, QUERY_HEADS * HEAD_SIZE), jnp.float32), -6.0, 6.0)
    return base_draw.astype(jnp.bfloat16)


def draw_key_value_cache(key, part):
    own_key = jax.random.fold_in(key, 47)
    whole_shape = (REQUEST_COUNT, 2, CACHE_SLOTS, KEY_VALUE_HEADS * HEAD_SIZE)
    base_draw = jnp.clip(jax.random.normal(own_key, whole_shape, jnp.float32), -6.0, 6.0)
    return base_draw.astype(jnp.bfloat16)


def draw_lengths(key, part):
    first_key, second_key = jax.random.split(jax.random.fold_in(key, 5))
    drawn_lengths = jax.random.randint(first_key, (REQUEST_COUNT,), CACHE_SLOTS // 4, CACHE_SLOTS + 1)
    chosen = jax.random.randint(second_key, (), 0, REQUEST_COUNT)
    drawn_lengths = drawn_lengths.at[chosen].set(CACHE_SLOTS)
    drawn_lengths = drawn_lengths.at[(chosen + 1) % REQUEST_COUNT].set(CACHE_SLOTS // 4)
    return drawn_lengths.astype(jnp.int32)


def draw_parents(key, part):
    node_index = jnp.arange(TREE_TOKENS, dtype=jnp.int32) % TREE_NODES
    chosen = jax.random.randint(jax.random.fold_in(key, 71), (TREE_TOKENS,), 0, jnp.maximum(node_index, 1))
    chained = jnp.maximum(node_index - 1, 0)
    return jnp.where(jnp.arange(TREE_TOKENS) < TREE_NODES, chained, chosen).astype(jnp.int32)


def touch_ends(values, key, smallest, top_value):
    extent = values.shape
    index_at = [jax.random.randint(jax.random.fold_in(key, axis), (), 0, extent[axis]) for axis in range(len(extent))]
    values = values.at[tuple(index_at)].set(smallest)
    longest = extent.index(max(extent))
    index_at[longest] = (index_at[longest] + 1) % extent[longest]
    return values.at[tuple(index_at)].set(top_value)


def steps_of(rng, dims, shards, smallest, high):
    def one(position, blocks):
        steps = jax.random.uniform(jax.random.fold_in(jax.random.fold_in(rng, 6), position), (blocks,), jnp.float32, smallest / len(shards), high / len(shards))
        return jnp.repeat(jnp.exp(steps), dims[position] // blocks).reshape((-1,) + (1,) * (len(dims) - position - 1))

    loudness = one(*shards[0])
    for cut in shards[1:]:
        loudness = loudness * one(*cut)
    return loudness


def routed_block(rng, own, number, rows, number_of, top, reach, skew):
    ranking = jax.random.permutation(rng, number_of)
    packed, ordinary = load_shares(number_of, rows * top, reach, skew, True), load_shares(number_of, rows * top, reach, skew, False)
    places = jnp.arange(number_of)

    def named(tallies, offset_by):
        used = int((tallies > 0).sum())
        fixed = max(1, used // 4)
        passed = fixed + (places - fixed + offset_by * (used - fixed)) % max(1, number_of - fixed)
        return jnp.zeros((number_of,), jnp.int32).at[ranking[jnp.where(places < fixed, places, passed)]].set(jnp.asarray(tallies, jnp.int32))

    tallies = jnp.where(number % 4 == 0, named(packed, number // 4), named(ordinary, number - number // 4 - 1))
    mixed = jax.random.permutation(jax.random.fold_in(own, 3), number_of)
    source_of, taker = mixed[0:number_of // 2 * 2:2], mixed[1:number_of // 2 * 2:2]
    room = jnp.minimum(tallies[source_of] - 1, reach - tallies[taker]) // 2
    room = jnp.where((source_of == ranking[0]) | (taker == ranking[0]) | (tallies[taker] == 0), 0, jnp.maximum(room, 0))
    passed = jax.random.randint(jax.random.fold_in(own, 4), (number_of // 2,), 0, 1 << 20) % (room + 1)
    tallies = tallies.at[source_of].add(-passed).at[taker].add(passed)
    members = jnp.searchsorted(jnp.cumsum(tallies), jnp.arange(rows * top), side="right").astype(jnp.int32)
    grid = members.reshape(top, rows).T
    grid = grid[jax.random.permutation(jax.random.fold_in(own, 1), rows)]
    offset_by = jax.random.randint(jax.random.fold_in(own, 2), (rows, 1), 0, top)
    return jnp.take_along_axis(grid, (jnp.arange(top)[None, :] + offset_by) % top, axis=1)


def load_shares(number_of, total, limit, slope, full):
    weights = [(1 << 20) // math.isqrt(standing ** slope) + 1 for standing in range(1, number_of + 1)]
    largest = limit if full else min(limit, max(-(-total // number_of), total * weights[0] // sum(weights)))
    least = 1 if total - largest >= number_of - 1 else 0
    given, surplus = [largest] + [least] * (number_of - 1), total - largest - least * (number_of - 1)
    while surplus > 0:
        free = [i for i in range(1, number_of) if given[i] < largest] or [i for i in range(1, number_of) if given[i] < limit]
        mass, left = sum([weights[i] for i in free]), surplus
        for i in free:
            addition = min(limit - given[i], max(1, left * weights[i] // mass), surplus)
            given[i] = given[i] + addition
            surplus = surplus - addition
    return np.array(given)


def centred(key, dims, width, reach, cuts=(), held_as=jnp.bfloat16):
    result = width * jax.random.normal(key, dims, jnp.float32)
    if cuts:
        result = result * steps_of(key, dims, cuts, -0.22, 0.18)
    return jnp.clip(result, -reach, reach).astype(held_as)


def setup_inputs(seed: int = 0, part: int = 0) -> dict:
    key_list = jax.random.split(jax.random.key(seed), 16)
    part_splits = jax.random.split(jax.random.fold_in(key_list[15], part), 16)
    queries = draw_queries(jax.random.fold_in(jax.random.fold_in(key_list[15], part), 71), part)
    tree_key_value = centred(part_splits[1], (TREE_TOKENS, 2, KEY_VALUE_HEADS * HEAD_SIZE), 1.0, 6.0, ((0, 16),))
    key_value_cache = draw_key_value_cache(jax.random.fold_in(jax.random.fold_in(key_list[15], part), 71), part)
    lengths = draw_lengths(jax.random.fold_in(jax.random.fold_in(key_list[15], part), 71), part)
    parents = draw_parents(jax.random.fold_in(jax.random.fold_in(key_list[15], part), 71), part)
    residual = centred(part_splits[5], (TREE_TOKENS, D), 1.0, 6.0, ((0, 16),))
    ffn_gain = jnp.clip(1.0 + 0.18 * jax.random.normal(key_list[6], (D,), jnp.float32), 0.099609375, 1.8984375).astype(jnp.bfloat16)
    router = centred(key_list[7], (D, EXPERTS), D ** -0.5, 0.078125)
    routes_keys = jax.random.split(jax.random.fold_in(part_splits[8], 1), TREE_TOKENS // TOK_DEV)
    routes_turns = jax.random.permutation(jax.random.fold_in(part_splits[8], 3), TREE_TOKENS // TOK_DEV)
    routes = jax.vmap(lambda own, number: routed_block(jax.random.fold_in(part_splits[8], 2), own, number, TOK_DEV, EXPERTS, 2, CAP, 2))(routes_keys, routes_turns).reshape((TREE_TOKENS, 2))
    gate_weight = centred(key_list[9], (D, EXPERTS * FF), D ** -0.5, 0.078125, ((1, 16),))
    up_weight = centred(key_list[10], (D, EXPERTS * FF), D ** -0.5, 0.078125, ((1, 16),))
    down_weight = centred(key_list[11], (EXPERTS * FF, D), FF ** -0.5, 0.0625, ((0, 16),))
    accepted = touch_ends(jax.random.randint(part_splits[12], (REQUEST_COUNT,), 0, TREE_NODES), jax.random.fold_in(part_splits[12], 1), 0, TREE_NODES - 1).astype(jnp.int32)
    next_embed = centred(part_splits[13], (REQUEST_COUNT, D), 1.0, 6.0, ((0, 16),))
    draft_fc = centred(key_list[14], (2 * D, D), (2 * D) ** -0.5, 0.0546875, ((0, 16),))
    return dict(queries=queries, tree_key_value=tree_key_value, key_value_cache=key_value_cache, lengths=lengths, parents=parents, residual=residual, ffn_gain=ffn_gain, router=router, routes=routes, gate_weight=gate_weight, up_weight=up_weight, down_weight=down_weight, accepted=accepted, next_embed=next_embed, draft_fc=draft_fc)


EPSILON = 1e-05

def round_trip(values):
    return lax.optimization_barrier(values.astype(jnp.bfloat16)).astype(jnp.float32)

def ancestors(parent_ids):
    node_ids = jnp.arange(TREE_NODES, dtype=jnp.int32)
    parent_map = (parent_ids[:, :, None] == node_ids[None, None, :]).astype(jnp.float32)
    current = jnp.broadcast_to(jnp.eye(TREE_NODES, dtype=jnp.float32), parent_map.shape)
    reached = current
    for repeat in range(TREE_NODES):
        current = jnp.einsum('rij,rjk->rik', current, parent_map, precision=lax.Precision.HIGHEST)
        reached = reached + current
    return reached > 0.5

def attention(queries, tree_key_value, key_value_cache, lengths, parents):
    request_total = lengths.shape[0]
    query_head_count = queries.astype(jnp.float32).reshape(request_total, TREE_NODES, KEY_VALUE_HEADS, QUERY_HEADS // KEY_VALUE_HEADS, HEAD_SIZE)
    cached_key_rows = key_value_cache[:, 0].astype(jnp.float32).reshape(request_total, CACHE_SLOTS, KEY_VALUE_HEADS, HEAD_SIZE)
    cached_value_rows = key_value_cache[:, 1].astype(jnp.float32).reshape(request_total, CACHE_SLOTS, KEY_VALUE_HEADS, HEAD_SIZE)
    tree_key_rows = tree_key_value[:, 0].astype(jnp.float32).reshape(request_total, TREE_NODES, KEY_VALUE_HEADS, HEAD_SIZE)
    tree_value_rows = tree_key_value[:, 1].astype(jnp.float32).reshape(request_total, TREE_NODES, KEY_VALUE_HEADS, HEAD_SIZE)
    score_scale = HEAD_SIZE ** (-0.5)
    cache_scores = jnp.einsum('rtgqd,rlgd->rgtql', query_head_count, cached_key_rows) * score_scale
    tree_scores = jnp.einsum('rtgqd,rugd->rgtqu', query_head_count, tree_key_rows) * score_scale
    visible = jnp.arange(CACHE_SLOTS, dtype=jnp.int32)[None, :] < lengths[:, None]
    related = ancestors(parents.reshape(request_total, TREE_NODES))
    cache_scores = jnp.where(visible[:, None, None, None, :], cache_scores, -1e+30)
    tree_scores = jnp.where(related[:, None, :, None, :], tree_scores, -1e+30)
    row_peak = jnp.maximum(lax.optimization_barrier(jnp.max(cache_scores, axis=-1)), lax.optimization_barrier(jnp.max(tree_scores, axis=-1)))[..., None]
    cache_exp = jnp.exp(cache_scores - row_peak)
    tree_exp = jnp.exp(tree_scores - row_peak)
    denominator = (lax.optimization_barrier(jnp.sum(cache_exp, axis=-1)) + lax.optimization_barrier(jnp.sum(tree_exp, axis=-1)))[..., None]
    cache_weights = round_trip(cache_exp / denominator)
    tree_weights = round_trip(tree_exp / denominator)
    context = jnp.einsum('rgtql,rlgd->rtgqd', cache_weights, cached_value_rows) + jnp.einsum('rgtqu,rugd->rtgqd', tree_weights, tree_value_rows)
    return context.reshape(request_total * TREE_NODES, QUERY_HEADS * HEAD_SIZE)

def reference(queries, tree_key_value, key_value_cache, lengths, parents, residual, ffn_gain, router, routes, gate_weight, up_weight, down_weight, accepted, next_embed, draft_fc):
    context = attention(queries, tree_key_value, key_value_cache, lengths, parents)
    hidden_state = residual.astype(jnp.float32) + context
    normed = (hidden_state * lax.rsqrt(lax.optimization_barrier(jnp.mean(hidden_state * hidden_state, axis=-1, keepdims=True)) + EPSILON) * ffn_gain.astype(jnp.float32)).astype(jnp.bfloat16)
    logits = jnp.dot(normed, router, preferred_element_type=jnp.float32)
    expert_ids = jnp.arange(EXPERTS, dtype=jnp.int32)
    first_hit = (routes[:, 0:1] == expert_ids[None, :]).astype(jnp.float32)
    second_hit = (routes[:, 1:2] == expert_ids[None, :]).astype(jnp.float32)
    first_logit = lax.optimization_barrier(jnp.sum(logits * first_hit, axis=-1))
    second_logit = lax.optimization_barrier(jnp.sum(logits * second_hit, axis=-1))
    first_share = jax.nn.sigmoid(first_logit - second_logit)
    mixing = first_share[:, None] * first_hit + (1.0 - first_share)[:, None] * second_hit
    shard_width = EXPERTS * FF // N_EXPERT
    group_size = N_EXPERT // EXPERTS

    def shard_step(running, shard_index):
        first_col = (shard_index * shard_width).astype(jnp.int32)
        gate_cols = lax.dynamic_slice_in_dim(gate_weight, first_col, shard_width, 1)
        up_cols = lax.dynamic_slice_in_dim(up_weight, first_col, shard_width, 1)
        down_rows = lax.dynamic_slice_in_dim(down_weight, first_col, shard_width, 0)
        gate_val = jnp.dot(normed, gate_cols, preferred_element_type=jnp.float32)
        up_val = jnp.dot(normed, up_cols, preferred_element_type=jnp.float32)
        activation = (jax.nn.silu(gate_val) * up_val).astype(jnp.bfloat16)
        partial_out = round_trip(jnp.dot(activation, down_rows, preferred_element_type=jnp.float32))
        mix_share = lax.dynamic_slice_in_dim(mixing, (shard_index // group_size).astype(jnp.int32), 1, 1)
        return (running + mix_share * partial_out, None)
    shard_ids = jnp.arange(N_EXPERT, dtype=jnp.int32)
    expert_sum, unused = lax.scan(shard_step, jnp.zeros(hidden_state.shape, jnp.float32), shard_ids)
    layer_out = (hidden_state + expert_sum).astype(jnp.bfloat16)
    request_total = lengths.shape[0]
    picker = (accepted[:, None] == jnp.arange(TREE_NODES, dtype=jnp.int32)[None, :]).astype(jnp.float32)
    picked = jnp.einsum('rt,rtd->rd', picker, layer_out.astype(jnp.float32).reshape(request_total, TREE_NODES, D)).astype(jnp.bfloat16)
    draft_in = jnp.concatenate([picked, next_embed], axis=1)
    draft_out = jnp.dot(draft_in, draft_fc, preferred_element_type=jnp.float32).astype(jnp.bfloat16)
    return (layer_out, draft_out)
```

```python
import functools

import jax
import jax.numpy as jnp
from jax import lax
from jax.experimental import pallas as pl
from jax.experimental.pallas import tpu as pltpu
from jax.sharding import PartitionSpec as P

QUERY_HEADS = 48
KEY_VALUE_HEADS = 8
HEAD_SIZE = 128
EXPERTS = 4
TREE_NODES = 6
CACHE_SLOTS = 512
CAP = 4


EPSILON = 1e-05


def ancestors(parent_ids):
    node_ids = jnp.arange(TREE_NODES, dtype=jnp.int32)
    parent_map = (parent_ids[:, :, None] == node_ids[None, None, :]).astype(jnp.float32)
    current = jnp.broadcast_to(jnp.eye(TREE_NODES, dtype=jnp.float32), parent_map.shape)
    reached = current
    for repeat in range(TREE_NODES):
        current = jnp.einsum("rij,rjk->rik", current, parent_map, precision=lax.Precision.HIGHEST)
        reached = reached + current
    return reached > 0.5


def attention(queries, tree_key_value, key_value_cache, lengths, parents):
    request_total = lengths.shape[0]
    query_head_count = queries.reshape(
        request_total, TREE_NODES, KEY_VALUE_HEADS, QUERY_HEADS // KEY_VALUE_HEADS, HEAD_SIZE
    )
    cached_key_rows = key_value_cache[:, 0].reshape(
        request_total, CACHE_SLOTS, KEY_VALUE_HEADS, HEAD_SIZE
    )
    cached_value_rows = key_value_cache[:, 1].reshape(
        request_total, CACHE_SLOTS, KEY_VALUE_HEADS, HEAD_SIZE
    )
    tree_key_rows = tree_key_value[:, 0].reshape(
        request_total, TREE_NODES, KEY_VALUE_HEADS, HEAD_SIZE
    )
    tree_value_rows = tree_key_value[:, 1].reshape(
        request_total, TREE_NODES, KEY_VALUE_HEADS, HEAD_SIZE
    )
    score_scale = HEAD_SIZE ** (-0.5)
    cache_scores = (
        jnp.einsum(
            "rtgqd,rlgd->rgtql",
            query_head_count,
            cached_key_rows,
            preferred_element_type=jnp.float32,
        )
        * score_scale
    )
    tree_scores = (
        jnp.einsum(
            "rtgqd,rugd->rgtqu", query_head_count, tree_key_rows, preferred_element_type=jnp.float32
        )
        * score_scale
    )
    visible = jnp.arange(CACHE_SLOTS, dtype=jnp.int32)[None, :] < lengths[:, None]
    related = ancestors(parents.reshape(request_total, TREE_NODES))
    cache_scores = jnp.where(visible[:, None, None, None, :], cache_scores, -1e30)
    tree_scores = jnp.where(related[:, None, :, None, :], tree_scores, -1e30)
    row_peak = jnp.maximum(jnp.max(cache_scores, axis=-1), jnp.max(tree_scores, axis=-1))[..., None]
    cache_exp = jnp.exp(cache_scores - row_peak)
    tree_exp = jnp.exp(tree_scores - row_peak)
    denominator = (jnp.sum(cache_exp, axis=-1) + jnp.sum(tree_exp, axis=-1))[..., None]
    cache_weights = (cache_exp / denominator).astype(jnp.bfloat16)
    tree_weights = (tree_exp / denominator).astype(jnp.bfloat16)
    context = jnp.einsum(
        "rgtql,rlgd->rtgqd", cache_weights, cached_value_rows, preferred_element_type=jnp.float32
    ) + jnp.einsum(
        "rgtqu,rugd->rtgqd", tree_weights, tree_value_rows, preferred_element_type=jnp.float32
    )
    return context.reshape(request_total * TREE_NODES, QUERY_HEADS * HEAD_SIZE)


VMEM_LIMIT = 66_000_000


def greet(n, me):
    barrier = pltpu.get_barrier_semaphore()

    def hello(k, carry):
        pl.semaphore_signal(barrier, inc=1, device_id={"expert": lax.rem(me + k, n)})
        return carry

    lax.fori_loop(1, n, hello, 0)
    pl.semaphore_wait(barrier, n - 1)


def push(src, dst, send_sem, recv_sem, peer):
    return pltpu.make_async_remote_copy(
        src_ref=src,
        dst_ref=dst,
        send_sem=send_sem,
        recv_sem=recv_sem,
        device_id={"expert": peer},
        device_id_type=pl.DeviceIdType.MESH,
    )


def moe_kernel(
    n,
    group_size,
    pair_slots,
    down_slots,
    packed,
    gate_hbm,
    up_hbm,
    down_hbm,
    grouped,
    gate_buf,
    up_buf,
    down_buf,
    arrived,
    rows_wide,
    rows,
    activation,
    result,
    leaving,
    returned,
    pair_sem,
    down_sem,
    out_sem,
    in_sem,
    back_out_sem,
    back_in_sem,
    own_sem,
):
    me = lax.axis_index("expert")
    width = gate_hbm.shape[1]
    chunk = gate_buf.shape[2]
    pair_count = width // chunk
    piece = down_buf.shape[2]
    piece_count = down_hbm.shape[1] // piece

    def pair_copies(i):
        slot = lax.rem(i, pair_slots)
        cols = pl.ds(pl.multiple_of(i * chunk, chunk), chunk)
        return (
            pltpu.make_async_copy(gate_hbm.at[:, cols], gate_buf.at[slot], pair_sem.at[0, slot]),
            pltpu.make_async_copy(up_hbm.at[:, cols], up_buf.at[slot], pair_sem.at[1, slot]),
        )

    def down_copy(i):
        slot = lax.rem(i, down_slots)
        cols = pl.ds(pl.multiple_of(i * piece, piece), piece)
        return pltpu.make_async_copy(down_hbm.at[:, cols], down_buf.at[slot], down_sem.at[slot])

    def start_pair(i, carry):
        for copy in pair_copies(i):
            copy.start()
        return carry

    def start_down(i, carry):
        down_copy(i).start()
        return carry

    lax.fori_loop(0, pair_slots, start_pair, 0)
    greet(n, me)

    def dispatch(k, carry):
        peer = lax.rem(me + k, n)
        push(
            packed.at[peer // group_size], arrived.at[me], out_sem.at[peer], in_sem.at[me], peer
        ).start()
        return carry

    lax.fori_loop(1, n, dispatch, 0)
    own = pltpu.make_async_copy(packed.at[me // group_size], arrived.at[me], own_sem)
    own.start()
    lax.fori_loop(0, down_slots, start_down, 0)
    own.wait()

    def take(k, carry):
        source = lax.rem(me + n - k, n)
        push(
            packed.at[0], arrived.at[source], out_sem.at[source], in_sem.at[source], source
        ).wait_recv()
        return carry

    lax.fori_loop(1, n, take, 0)

    def both(pair):
        return pl.ds(pl.multiple_of(pair * 2 * CAP, 2 * CAP), 2 * CAP)

    def widen(pair, carry):
        rows_wide[both(pair), :] = jnp.concatenate(
            [arrived[2 * pair].astype(jnp.float32), arrived[2 * pair + 1].astype(jnp.float32)],
            axis=0,
        )
        return carry

    lax.fori_loop(0, n // 2, widen, 0)
    rows[...] = rows_wide[...].astype(jnp.bfloat16)

    def pair_step(i, carry):
        slot = lax.rem(i, pair_slots)
        for copy in pair_copies(i):
            copy.wait()
        gate_val = jnp.dot(rows[...], gate_buf[slot], preferred_element_type=jnp.float32)
        up_val = jnp.dot(rows[...], up_buf[slot], preferred_element_type=jnp.float32)
        cols = pl.ds(pl.multiple_of(i * chunk, chunk), chunk)
        activation[:, cols] = (jax.nn.silu(gate_val) * up_val).astype(jnp.bfloat16)

        @pl.when(i + pair_slots < pair_count)
        def _():
            start_pair(i + pair_slots, 0)

        return carry

    lax.fori_loop(0, pair_count, pair_step, 0)

    def down_step(i, carry):
        slot = lax.rem(i, down_slots)
        down_copy(i).wait()
        result[...] = jnp.dot(
            activation[...], down_buf[slot], preferred_element_type=jnp.float32
        )

        @pl.when(i + down_slots < piece_count)
        def _():
            start_down(i + down_slots, 0)

        def narrow(pair, inner):
            block = result[both(pair), :]
            leaving[2 * pair, i] = block[:CAP].astype(jnp.bfloat16)
            leaving[2 * pair + 1, i] = block[CAP:].astype(jnp.bfloat16)
            return inner

        lax.fori_loop(0, n // 2, narrow, 0)

        def send_back(k, inner):
            peer = lax.rem(me + k, n)
            push(
                leaving.at[peer, i],
                returned.at[me, i],
                back_out_sem.at[peer],
                back_in_sem.at[me],
                peer,
            ).start()
            return inner

        lax.fori_loop(1, n, send_back, 0)
        return carry

    lax.fori_loop(0, piece_count, down_step, 0)
    returned[me] = leaving[me]

    def drain(k, carry):
        peer = lax.rem(me + n - k, n)
        push(
            leaving.at[peer], returned.at[peer], back_out_sem.at[peer], back_in_sem.at[peer], peer
        ).wait()
        push(
            packed.at[0], arrived.at[peer], out_sem.at[peer], in_sem.at[peer], peer
        ).wait_send()
        return carry

    lax.fori_loop(1, n, drain, 0)

    def gather(expert, carry):
        for i in range(piece_count):

            def add(member, total):
                return total + returned[expert * group_size + member, i].astype(jnp.float32)

            grouped[expert, :, i * piece : (i + 1) * piece] = lax.fori_loop(
                0, group_size, add, jnp.zeros((CAP, piece), jnp.float32)
            )
        return carry

    lax.fori_loop(0, EXPERTS, gather, 0)


def moe(packed, gate_weight, up_weight, down_weight, n):
    model_width, width = gate_weight.shape
    row_count = n * CAP
    chunk = min(256, width)
    piece = model_width // 4
    pair_slots = min(5, width // chunk)
    down_slots = min(3, model_width // piece)
    anywhere = pl.BlockSpec(memory_space=pl.ANY)
    whole = pl.BlockSpec(memory_space=pltpu.VMEM)
    bf16, f32 = jnp.bfloat16, jnp.float32
    return pl.pallas_call(
        functools.partial(moe_kernel, n, n // EXPERTS, pair_slots, down_slots),
        out_shape=jax.ShapeDtypeStruct((EXPERTS, CAP, model_width), f32),
        in_specs=[whole, anywhere, anywhere, anywhere],
        out_specs=whole,
        scratch_shapes=[
            pltpu.VMEM((pair_slots, model_width, chunk), bf16),
            pltpu.VMEM((pair_slots, model_width, chunk), bf16),
            pltpu.VMEM((down_slots, width, piece), bf16),
            pltpu.VMEM((n, CAP, model_width), bf16),
            pltpu.VMEM((row_count, model_width), f32),
            pltpu.VMEM((row_count, model_width), bf16),
            pltpu.VMEM((row_count, width), bf16),
            pltpu.VMEM((row_count, piece), f32),
            pltpu.VMEM((n, model_width // piece, CAP, piece), bf16),
            pltpu.VMEM((n, model_width // piece, CAP, piece), bf16),
            pltpu.SemaphoreType.DMA((2, pair_slots)),
            pltpu.SemaphoreType.DMA((down_slots,)),
            pltpu.SemaphoreType.DMA((n,)),
            pltpu.SemaphoreType.DMA((n,)),
            pltpu.SemaphoreType.DMA((n,)),
            pltpu.SemaphoreType.DMA((n,)),
            pltpu.SemaphoreType.DMA,
        ],
        compiler_params=pltpu.CompilerParams(
            collective_id=0, has_side_effects=True, vmem_limit_bytes=VMEM_LIMIT
        ),
        name="moe",
    )(packed, gate_weight, up_weight, down_weight)


def draft_kernel(
    n,
    share,
    piece,
    blocks,
    fc_hbm,
    out,
    fc_buf,
    arrived,
    rows_wide,
    result,
    leaving,
    returned,
    fc_sem,
    out_sem,
    in_sem,
    back_out_sem,
    back_in_sem,
):
    me = lax.axis_index("expert")
    piece_count = fc_hbm.shape[1] // piece

    def fc_copy(i):
        cols = pl.ds(pl.multiple_of(i * piece, piece), piece)
        return pltpu.make_async_copy(fc_hbm.at[:, cols], fc_buf.at[i], fc_sem.at[i])

    def start_fc(i, carry):
        fc_copy(i).start()
        return carry

    lax.fori_loop(0, piece_count, start_fc, 0)
    greet(n, me)

    def dispatch(k, carry):
        peer = lax.rem(me + k, n)
        push(blocks.at[peer], arrived.at[me], out_sem.at[peer], in_sem.at[me], peer).start()
        return carry

    lax.fori_loop(1, n, dispatch, 0)
    rows_wide[pl.ds(me * share, share), :] = blocks[me]

    def take(k, carry):
        source = lax.rem(me + n - k, n)
        push(
            blocks.at[source], arrived.at[source], out_sem.at[source], in_sem.at[source], source
        ).wait()
        rows_wide[pl.ds(source * share, share), :] = arrived[source]
        return carry

    lax.fori_loop(1, n, take, 0)

    def step(i, carry):
        fc_copy(i).wait()
        result[...] = jnp.dot(
            rows_wide[...].astype(jnp.bfloat16), fc_buf[i], preferred_element_type=jnp.float32
        )

        def split(source, inner):
            leaving[source, i] = result[pl.ds(source * share, share), :]
            return inner

        lax.fori_loop(0, n, split, 0)

        def send_back(k, inner):
            peer = lax.rem(me + k, n)
            push(
                leaving.at[peer, i],
                returned.at[me, i],
                back_out_sem.at[peer],
                back_in_sem.at[me],
                peer,
            ).start()
            return inner

        lax.fori_loop(1, n, send_back, 0)
        return carry

    lax.fori_loop(0, piece_count, step, 0)
    returned[me] = leaving[me]

    def drain(k, carry):
        peer = lax.rem(me + n - k, n)
        push(
            leaving.at[peer], returned.at[peer], back_out_sem.at[peer], back_in_sem.at[peer], peer
        ).wait()
        return carry

    lax.fori_loop(1, n, drain, 0)
    for i in range(piece_count):

        def add(source, total):
            return total + returned[source, i]

        out[:, i * piece : (i + 1) * piece] = lax.fori_loop(
            0, n, add, jnp.zeros((share, piece), jnp.float32)
        ).astype(out.dtype)


def draft(blocks, draft_fc):
    n, share, depth = blocks.shape
    model_width = draft_fc.shape[1]
    piece = model_width // 4
    pieces = model_width // piece
    whole = pl.BlockSpec(memory_space=pltpu.VMEM)
    f32 = jnp.float32
    return pl.pallas_call(
        functools.partial(draft_kernel, n, share, piece),
        out_shape=jax.ShapeDtypeStruct((share, model_width), jnp.bfloat16),
        in_specs=[whole, pl.BlockSpec(memory_space=pl.ANY)],
        out_specs=whole,
        scratch_shapes=[
            pltpu.VMEM((pieces, depth, piece), jnp.bfloat16),
            pltpu.VMEM((n, share, depth), f32),
            pltpu.VMEM((n * share, depth), f32),
            pltpu.VMEM((n * share, piece), f32),
            pltpu.VMEM((n, pieces, share, piece), f32),
            pltpu.VMEM((n, pieces, share, piece), f32),
            pltpu.SemaphoreType.DMA((pieces,)),
            pltpu.SemaphoreType.DMA((n,)),
            pltpu.SemaphoreType.DMA((n,)),
            pltpu.SemaphoreType.DMA((n,)),
            pltpu.SemaphoreType.DMA((n,)),
        ],
        compiler_params=pltpu.CompilerParams(
            collective_id=1, has_side_effects=True, vmem_limit_bytes=VMEM_LIMIT
        ),
        name="draft",
    )(blocks, draft_fc)


def per_device(
    queries,
    tree_key_value,
    key_value_cache,
    lengths,
    parents,
    residual,
    ffn_gain,
    router,
    routes,
    gate_weight,
    up_weight,
    down_weight,
    accepted,
    next_embed,
    draft_fc,
):
    devices = lax.axis_size("expert")
    context = attention(queries, tree_key_value, key_value_cache, lengths, parents)
    hidden_state = residual.astype(jnp.float32) + context
    normed = (
        hidden_state
        * lax.rsqrt(jnp.mean(hidden_state * hidden_state, axis=-1, keepdims=True) + EPSILON)
        * ffn_gain.astype(jnp.float32)
    ).astype(jnp.bfloat16)
    tokens_here, model_width = normed.shape
    logits = jnp.dot(normed, router, preferred_element_type=jnp.float32)
    expert_ids = jnp.arange(EXPERTS, dtype=jnp.int32)
    first_hit = (routes[:, 0:1] == expert_ids[None, :]).astype(jnp.float32)
    second_hit = (routes[:, 1:2] == expert_ids[None, :]).astype(jnp.float32)
    first_logit = jnp.sum(logits * first_hit, axis=-1)
    second_logit = jnp.sum(logits * second_hit, axis=-1)
    first_share = jax.nn.sigmoid(first_logit - second_logit)
    mixing = first_share[:, None] * first_hit + (1.0 - first_share)[:, None] * second_hit
    hit_table = first_hit + second_hit
    slot_rank = jnp.cumsum(hit_table, axis=0) - 1.0
    slot_ids = jnp.arange(CAP, dtype=jnp.float32)
    placing = hit_table.T[:, None, :] * (slot_rank.T[:, None, :] == slot_ids[None, :, None]).astype(
        jnp.float32
    )
    packed = jnp.einsum(
        "ect,td->ecd", placing.astype(jnp.bfloat16), normed, preferred_element_type=jnp.float32
    ).astype(jnp.bfloat16)
    grouped = moe(packed, gate_weight, up_weight, down_weight, devices)
    weighted = placing * mixing.T[:, None, :]
    expert_sum = jnp.einsum("ect,ecd->td", weighted, grouped, precision=lax.Precision.HIGHEST)
    layer_out = (hidden_state + expert_sum).astype(jnp.bfloat16)
    request_total = lengths.shape[0]
    picker = (accepted[:, None] == jnp.arange(TREE_NODES, dtype=jnp.int32)[None, :]).astype(
        jnp.bfloat16
    )
    picked = jnp.einsum(
        "rt,rtd->rd",
        picker,
        layer_out.reshape(request_total, TREE_NODES, model_width),
        preferred_element_type=jnp.float32,
    ).astype(jnp.bfloat16)
    draft_in = jnp.concatenate([picked, next_embed], axis=1)
    depth = draft_fc.shape[0]
    blocks = draft_in.reshape(request_total, devices, depth).transpose(1, 0, 2)
    draft_out = draft(blocks.astype(jnp.float32), draft_fc)
    return (layer_out, draft_out)


def solution(mesh):
    return jax.shard_map(
        per_device,
        mesh=mesh,
        in_specs=(
            P(("groups", "expert"), None),
            P(("groups", "expert"), None, None),
            P(("groups", "expert"), None, None, None),
            P(("groups", "expert")),
            P(("groups", "expert")),
            P(("groups", "expert"), None),
            P(),
            P(),
            P(("groups", "expert"), None),
            P(None, "expert"),
            P(None, "expert"),
            P("expert", None),
            P(("groups", "expert")),
            P(("groups", "expert"), None),
            P("expert", None),
        ),
        out_specs=(P(("groups", "expert"), None), P(("groups", "expert"), None)),
        check_vma=False,
    )
```

```python
import functools

import jax
import jax.numpy as jnp
from jax import lax
from jax.experimental import pallas as pl
from jax.experimental.pallas import tpu as pltpu
from jax.sharding import PartitionSpec as P

QUERY_HEADS = 48
KEY_VALUE_HEADS = 8
HEAD_SIZE = 128
EXPERTS = 4
TREE_NODES = 6
CACHE_SLOTS = 512
CAP = 4


EPSILON = 1e-05


def related_kernel(parents, out):
    node_ids = lax.broadcasted_iota(jnp.int32, (1, out.shape[2]), 1)
    for request in range(out.shape[0]):
        reached = []
        for node in range(TREE_NODES):
            row = (node_ids == node).astype(jnp.float32)
            parent = parents[request * TREE_NODES + node]
            for earlier in range(node):
                row = row + jnp.where(parent == earlier, reached[earlier], 0.0)
            reached.append(row)
            out[request, node : node + 1, :] = row


def ancestors(parent_ids):
    table = pl.pallas_call(
        related_kernel,
        out_shape=jax.ShapeDtypeStruct((parent_ids.shape[0] // TREE_NODES, TREE_NODES, 128), jnp.float32),
        in_specs=[pl.BlockSpec(memory_space=pltpu.SMEM)],
        out_specs=pl.BlockSpec(memory_space=pltpu.VMEM),
        name="related",
    )(parent_ids)
    return table[:, :, :TREE_NODES] > 0.5


def attention(queries, tree_key_value, key_value_cache, lengths, parents):
    request_total = lengths.shape[0]
    query_head_count = queries.reshape(
        request_total, TREE_NODES, KEY_VALUE_HEADS, QUERY_HEADS // KEY_VALUE_HEADS, HEAD_SIZE
    )
    cached_key_rows = key_value_cache[:, 0].reshape(
        request_total, CACHE_SLOTS, KEY_VALUE_HEADS, HEAD_SIZE
    )
    cached_value_rows = key_value_cache[:, 1].reshape(
        request_total, CACHE_SLOTS, KEY_VALUE_HEADS, HEAD_SIZE
    )
    tree_key_rows = tree_key_value[:, 0].reshape(
        request_total, TREE_NODES, KEY_VALUE_HEADS, HEAD_SIZE
    )
    tree_value_rows = tree_key_value[:, 1].reshape(
        request_total, TREE_NODES, KEY_VALUE_HEADS, HEAD_SIZE
    )
    score_scale = HEAD_SIZE ** (-0.5)
    cache_scores = (
        jnp.einsum(
            "rtgqd,rlgd->rgtql",
            query_head_count,
            cached_key_rows,
            preferred_element_type=jnp.float32,
        )
        * score_scale
    )
    tree_scores = (
        jnp.einsum(
            "rtgqd,rugd->rgtqu", query_head_count, tree_key_rows, preferred_element_type=jnp.float32
        )
        * score_scale
    )
    visible = jnp.arange(CACHE_SLOTS, dtype=jnp.int32)[None, :] < lengths[:, None]
    related = ancestors(parents)
    cache_scores = jnp.where(visible[:, None, None, None, :], cache_scores, -1e30)
    tree_scores = jnp.where(related[:, None, :, None, :], tree_scores, -1e30)
    row_peak = jnp.maximum(jnp.max(cache_scores, axis=-1), jnp.max(tree_scores, axis=-1))[..., None]
    cache_exp = jnp.exp(cache_scores - row_peak)
    tree_exp = jnp.exp(tree_scores - row_peak)
    denominator = (jnp.sum(cache_exp, axis=-1) + jnp.sum(tree_exp, axis=-1))[..., None]
    cache_weights = (cache_exp / denominator).astype(jnp.bfloat16)
    tree_weights = (tree_exp / denominator).astype(jnp.bfloat16)
    context = jnp.einsum(
        "rgtql,rlgd->rtgqd", cache_weights, cached_value_rows, preferred_element_type=jnp.float32
    ) + jnp.einsum(
        "rgtqu,rugd->rtgqd", tree_weights, tree_value_rows, preferred_element_type=jnp.float32
    )
    return context.reshape(request_total * TREE_NODES, QUERY_HEADS * HEAD_SIZE)


VMEM_LIMIT = 66_000_000


def greet(n, me):
    barrier = pltpu.get_barrier_semaphore()

    def hello(k, carry):
        pl.semaphore_signal(barrier, inc=1, device_id={"expert": lax.rem(me + k, n)})
        return carry

    lax.fori_loop(1, n, hello, 0)
    pl.semaphore_wait(barrier, n - 1)


def push(src, dst, send_sem, recv_sem, peer):
    return pltpu.make_async_remote_copy(
        src_ref=src,
        dst_ref=dst,
        send_sem=send_sem,
        recv_sem=recv_sem,
        device_id={"expert": peer},
        device_id_type=pl.DeviceIdType.MESH,
    )


def moe_kernel(
    n,
    group_size,
    pair_slots,
    down_slots,
    packed,
    gate_hbm,
    up_hbm,
    down_hbm,
    grouped,
    gate_buf,
    up_buf,
    down_buf,
    arrived,
    rows_wide,
    rows,
    activation,
    result,
    leaving,
    returned,
    pair_sem,
    down_sem,
    out_sem,
    in_sem,
    back_out_sem,
    back_in_sem,
    own_sem,
):
    me = lax.axis_index("expert")
    width = gate_hbm.shape[1]
    chunk = gate_buf.shape[2]
    pair_count = width // chunk
    piece = down_buf.shape[2]
    piece_count = down_hbm.shape[1] // piece

    def pair_copies(i):
        slot = lax.rem(i, pair_slots)
        cols = pl.ds(pl.multiple_of(i * chunk, chunk), chunk)
        return (
            pltpu.make_async_copy(gate_hbm.at[:, cols], gate_buf.at[slot], pair_sem.at[0, slot]),
            pltpu.make_async_copy(up_hbm.at[:, cols], up_buf.at[slot], pair_sem.at[1, slot]),
        )

    def down_copy(i):
        slot = lax.rem(i, down_slots)
        cols = pl.ds(pl.multiple_of(i * piece, piece), piece)
        return pltpu.make_async_copy(down_hbm.at[:, cols], down_buf.at[slot], down_sem.at[slot])

    def start_pair(i, carry):
        for copy in pair_copies(i):
            copy.start()
        return carry

    def start_down(i, carry):
        down_copy(i).start()
        return carry

    lax.fori_loop(0, pair_slots, start_pair, 0)
    greet(n, me)

    def dispatch(k, carry):
        peer = lax.rem(me + k, n)
        push(
            packed.at[peer // group_size], arrived.at[me], out_sem.at[peer], in_sem.at[me], peer
        ).start()
        return carry

    lax.fori_loop(1, n, dispatch, 0)
    own = pltpu.make_async_copy(packed.at[me // group_size], arrived.at[me], own_sem)
    own.start()
    lax.fori_loop(0, down_slots, start_down, 0)
    own.wait()

    def take(k, carry):
        source = lax.rem(me + n - k, n)
        push(
            packed.at[0], arrived.at[source], out_sem.at[source], in_sem.at[source], source
        ).wait_recv()
        return carry

    lax.fori_loop(1, n, take, 0)

    def both(pair):
        return pl.ds(pl.multiple_of(pair * 2 * CAP, 2 * CAP), 2 * CAP)

    def widen(pair, carry):
        rows_wide[both(pair), :] = jnp.concatenate(
            [arrived[2 * pair].astype(jnp.float32), arrived[2 * pair + 1].astype(jnp.float32)],
            axis=0,
        )
        return carry

    lax.fori_loop(0, n // 2, widen, 0)
    rows[...] = rows_wide[...].astype(jnp.bfloat16)

    def pair_step(i, carry):
        slot = lax.rem(i, pair_slots)
        for copy in pair_copies(i):
            copy.wait()
        gate_val = jnp.dot(rows[...], gate_buf[slot], preferred_element_type=jnp.float32)
        up_val = jnp.dot(rows[...], up_buf[slot], preferred_element_type=jnp.float32)
        cols = pl.ds(pl.multiple_of(i * chunk, chunk), chunk)
        activation[:, cols] = (jax.nn.silu(gate_val) * up_val).astype(jnp.bfloat16)

        @pl.when(i + pair_slots < pair_count)
        def _():
            start_pair(i + pair_slots, 0)

        return carry

    lax.fori_loop(0, pair_count, pair_step, 0)

    def down_step(i, carry):
        slot = lax.rem(i, down_slots)
        down_copy(i).wait()
        result[...] = jnp.dot(
            activation[...], down_buf[slot], preferred_element_type=jnp.float32
        )

        @pl.when(i + down_slots < piece_count)
        def _():
            start_down(i + down_slots, 0)

        def narrow(pair, inner):
            block = result[both(pair), :]
            leaving[2 * pair, i] = block[:CAP].astype(jnp.bfloat16)
            leaving[2 * pair + 1, i] = block[CAP:].astype(jnp.bfloat16)
            return inner

        lax.fori_loop(0, n // 2, narrow, 0)

        def send_back(k, inner):
            peer = lax.rem(me + k, n)
            push(
                leaving.at[peer, i],
                returned.at[me, i],
                back_out_sem.at[peer],
                back_in_sem.at[me],
                peer,
            ).start()
            return inner

        lax.fori_loop(1, n, send_back, 0)
        return carry

    lax.fori_loop(0, piece_count, down_step, 0)
    returned[me] = leaving[me]

    def drain(k, carry):
        peer = lax.rem(me + n - k, n)
        push(
            leaving.at[peer], returned.at[peer], back_out_sem.at[peer], back_in_sem.at[peer], peer
        ).wait()
        push(
            packed.at[0], arrived.at[peer], out_sem.at[peer], in_sem.at[peer], peer
        ).wait_send()
        return carry

    lax.fori_loop(1, n, drain, 0)

    def gather(expert, carry):
        for i in range(piece_count):

            def add(member, total):
                return total + returned[expert * group_size + member, i].astype(jnp.float32)

            grouped[expert, :, i * piece : (i + 1) * piece] = lax.fori_loop(
                0, group_size, add, jnp.zeros((CAP, piece), jnp.float32)
            )
        return carry

    lax.fori_loop(0, EXPERTS, gather, 0)


def moe(packed, gate_weight, up_weight, down_weight, n):
    model_width, width = gate_weight.shape
    row_count = n * CAP
    chunk = min(512, width)
    piece = model_width // 4
    pair_slots = min(3, width // chunk)
    down_slots = min(2, model_width // piece)
    anywhere = pl.BlockSpec(memory_space=pl.ANY)
    whole = pl.BlockSpec(memory_space=pltpu.VMEM)
    bf16, f32 = jnp.bfloat16, jnp.float32
    return pl.pallas_call(
        functools.partial(moe_kernel, n, n // EXPERTS, pair_slots, down_slots),
        out_shape=jax.ShapeDtypeStruct((EXPERTS, CAP, model_width), f32),
        in_specs=[whole, anywhere, anywhere, anywhere],
        out_specs=whole,
        scratch_shapes=[
            pltpu.VMEM((pair_slots, model_width, chunk), bf16),
            pltpu.VMEM((pair_slots, model_width, chunk), bf16),
            pltpu.VMEM((down_slots, width, piece), bf16),
            pltpu.VMEM((n, CAP, model_width), bf16),
            pltpu.VMEM((row_count, model_width), f32),
            pltpu.VMEM((row_count, model_width), bf16),
            pltpu.VMEM((row_count, width), bf16),
            pltpu.VMEM((row_count, piece), f32),
            pltpu.VMEM((n, model_width // piece, CAP, piece), bf16),
            pltpu.VMEM((n, model_width // piece, CAP, piece), bf16),
            pltpu.SemaphoreType.DMA((2, pair_slots)),
            pltpu.SemaphoreType.DMA((down_slots,)),
            pltpu.SemaphoreType.DMA((n,)),
            pltpu.SemaphoreType.DMA((n,)),
            pltpu.SemaphoreType.DMA((n,)),
            pltpu.SemaphoreType.DMA((n,)),
            pltpu.SemaphoreType.DMA,
        ],
        compiler_params=pltpu.CompilerParams(
            collective_id=0, has_side_effects=True, vmem_limit_bytes=VMEM_LIMIT
        ),
        name="moe",
    )(packed, gate_weight, up_weight, down_weight)


def draft_kernel(
    n,
    share,
    piece,
    blocks,
    fc_hbm,
    out,
    fc_buf,
    arrived,
    rows_wide,
    result,
    leaving,
    returned,
    fc_sem,
    out_sem,
    in_sem,
    back_out_sem,
    back_in_sem,
):
    me = lax.axis_index("expert")
    piece_count = fc_hbm.shape[1] // piece
    half = piece // 2

    def fc_copy(i):
        cols = pl.ds(pl.multiple_of(i * piece, piece), piece)
        return pltpu.make_async_copy(fc_hbm.at[:, cols], fc_buf.at[i], fc_sem.at[i])

    def start_fc(i, carry):
        fc_copy(i).start()
        return carry

    lax.fori_loop(0, piece_count, start_fc, 0)
    greet(n, me)

    def dispatch(k, carry):
        peer = lax.rem(me + k, n)
        push(blocks.at[peer], arrived.at[me], out_sem.at[peer], in_sem.at[me], peer).start()
        return carry

    lax.fori_loop(1, n, dispatch, 0)
    rows_wide[pl.ds(me * share, share), :] = blocks[me]

    def take(k, carry):
        source = lax.rem(me + n - k, n)
        push(
            blocks.at[source], arrived.at[source], out_sem.at[source], in_sem.at[source], source
        ).wait()
        rows_wide[pl.ds(source * share, share), :] = arrived[source]
        return carry

    lax.fori_loop(1, n, take, 0)

    def step(i, carry):
        fc_copy(i).wait()
        result[...] = jnp.dot(
            rows_wide[...].astype(jnp.bfloat16), fc_buf[i], preferred_element_type=jnp.float32
        )

        def split(source, inner):
            block = result[pl.ds(source * share, share), :]
            leaving[source, i] = jnp.concatenate(
                [block[:, :half], block[:, half:]], axis=0
            ).astype(jnp.bfloat16)
            return inner

        lax.fori_loop(0, n, split, 0)

        def send_back(k, inner):
            peer = lax.rem(me + k, n)
            push(
                leaving.at[peer, i],
                returned.at[me, i],
                back_out_sem.at[peer],
                back_in_sem.at[me],
                peer,
            ).start()
            return inner

        lax.fori_loop(1, n, send_back, 0)
        return carry

    lax.fori_loop(0, piece_count, step, 0)
    returned[me] = leaving[me]

    def drain(k, carry):
        peer = lax.rem(me + n - k, n)
        push(
            leaving.at[peer], returned.at[peer], back_out_sem.at[peer], back_in_sem.at[peer], peer
        ).wait()
        return carry

    lax.fori_loop(1, n, drain, 0)
    for i in range(piece_count):

        def add(source, total):
            return total + returned[source, i].astype(jnp.float32)

        total = lax.fori_loop(0, n, add, jnp.zeros((2 * share, half), jnp.float32))
        out[:, i * piece : i * piece + half] = total[:share]
        out[:, i * piece + half : (i + 1) * piece] = total[share:]


def draft(blocks, draft_fc):
    n, share, depth = blocks.shape
    model_width = draft_fc.shape[1]
    piece = model_width // 4
    pieces = model_width // piece
    whole = pl.BlockSpec(memory_space=pltpu.VMEM)
    f32 = jnp.float32
    return pl.pallas_call(
        functools.partial(draft_kernel, n, share, piece),
        out_shape=jax.ShapeDtypeStruct((share, model_width), f32),
        in_specs=[whole, pl.BlockSpec(memory_space=pl.ANY)],
        out_specs=whole,
        scratch_shapes=[
            pltpu.VMEM((pieces, depth, piece), jnp.bfloat16),
            pltpu.VMEM((n, share, depth), f32),
            pltpu.VMEM((n * share, depth), f32),
            pltpu.VMEM((n * share, piece), f32),
            pltpu.VMEM((n, pieces, 2 * share, piece // 2), jnp.bfloat16),
            pltpu.VMEM((n, pieces, 2 * share, piece // 2), jnp.bfloat16),
            pltpu.SemaphoreType.DMA((pieces,)),
            pltpu.SemaphoreType.DMA((n,)),
            pltpu.SemaphoreType.DMA((n,)),
            pltpu.SemaphoreType.DMA((n,)),
            pltpu.SemaphoreType.DMA((n,)),
        ],
        compiler_params=pltpu.CompilerParams(
            collective_id=1, has_side_effects=True, vmem_limit_bytes=VMEM_LIMIT
        ),
        name="draft",
    )(blocks, draft_fc)


def per_device(
    queries,
    tree_key_value,
    key_value_cache,
    lengths,
    parents,
    residual,
    ffn_gain,
    router,
    routes,
    gate_weight,
    up_weight,
    down_weight,
    accepted,
    next_embed,
    draft_fc,
):
    devices = lax.axis_size("expert")
    context = attention(queries, tree_key_value, key_value_cache, lengths, parents)
    hidden_state = residual.astype(jnp.float32) + context
    normed = (
        hidden_state
        * lax.rsqrt(jnp.mean(hidden_state * hidden_state, axis=-1, keepdims=True) + EPSILON)
        * ffn_gain.astype(jnp.float32)
    ).astype(jnp.bfloat16)
    tokens_here, model_width = normed.shape
    logits = jnp.dot(normed, router, preferred_element_type=jnp.float32)
    expert_ids = jnp.arange(EXPERTS, dtype=jnp.int32)
    first_hit = (routes[:, 0:1] == expert_ids[None, :]).astype(jnp.float32)
    second_hit = (routes[:, 1:2] == expert_ids[None, :]).astype(jnp.float32)
    first_logit = jnp.sum(logits * first_hit, axis=-1)
    second_logit = jnp.sum(logits * second_hit, axis=-1)
    first_share = jax.nn.sigmoid(first_logit - second_logit)
    mixing = first_share[:, None] * first_hit + (1.0 - first_share)[:, None] * second_hit
    hit_table = first_hit + second_hit
    slot_rank = jnp.cumsum(hit_table, axis=0) - 1.0
    slot_ids = jnp.arange(CAP, dtype=jnp.float32)
    placing = hit_table.T[:, None, :] * (slot_rank.T[:, None, :] == slot_ids[None, :, None]).astype(
        jnp.float32
    )
    packed = jnp.einsum(
        "ect,td->ecd", placing.astype(jnp.bfloat16), normed, preferred_element_type=jnp.float32
    ).astype(jnp.bfloat16)
    grouped = moe(packed, gate_weight, up_weight, down_weight, devices)
    weighted = placing * mixing.T[:, None, :]
    expert_sum = jnp.einsum("ect,ecd->td", weighted, grouped, precision=lax.Precision.HIGHEST)
    layer_out = (hidden_state + expert_sum).astype(jnp.bfloat16)
    request_total = lengths.shape[0]
    picker = (accepted[:, None] == jnp.arange(TREE_NODES, dtype=jnp.int32)[None, :]).astype(
        jnp.bfloat16
    )
    picked = jnp.einsum(
        "rt,rtd->rd",
        picker,
        layer_out.reshape(request_total, TREE_NODES, model_width),
        preferred_element_type=jnp.float32,
    ).astype(jnp.bfloat16)
    draft_in = jnp.concatenate([picked, next_embed], axis=1)
    depth = draft_fc.shape[0]
    blocks = draft_in.reshape(request_total, devices, depth).transpose(1, 0, 2)
    draft_out = draft(blocks.astype(jnp.float32), draft_fc).astype(jnp.bfloat16)
    return (layer_out, draft_out)


def solution(mesh):
    return jax.shard_map(
        per_device,
        mesh=mesh,
        in_specs=(
            P(("groups", "expert"), None),
            P(("groups", "expert"), None, None),
            P(("groups", "expert"), None, None, None),
            P(("groups", "expert")),
            P(("groups", "expert")),
            P(("groups", "expert"), None),
            P(),
            P(),
            P(("groups", "expert"), None),
            P(None, "expert"),
            P(None, "expert"),
            P("expert", None),
            P(("groups", "expert")),
            P(("groups", "expert"), None),
            P("expert", None),
        ),
        out_specs=(P(("groups", "expert"), None), P(("groups", "expert"), None)),
        check_vma=False,
    )
```
